32 devices in a mesh: ctx: 8 (over z, core), tp: 4 (over y, x).
Axes of the slice: x: 2, y: 2, z: 4, core: 2. Of those that a mesh axis runs over, the one named last changes fastest.
Arguments:
- queries: bfloat16 [2048, 4096], P('ctx', 'tp'), may hold values from -6 to 6
- key_rows: bfloat16 [2048, 4096], P('ctx', 'tp'), may hold values from -6 to 6
- value_rows: bfloat16 [2048, 4096], P('ctx', 'tp'), may hold values from -6 to 6
- segment_ids: int32 [2048], replicated, may hold values from 0 to 3, never falling along the last dimension, each value on 1 to 1024 neighbouring positions
- codebook_ids: int32 [2048, 8], P(('ctx', 'tp')), may hold values from 0 to 2047
- code_table: bfloat16 [8, 2048, 1024], P(None, 'tp'), may hold values from -4 to 4
- input_proj: bfloat16 [4096, 1024], replicated, may hold values from -0.75 to 0.75
- norm_gain: float32 [1024], replicated, may hold values from 0.1 to 1.9
- upstream: bfloat16 [2048, 8, 1024], P(('ctx', 'tp')), may hold values from -3 to 3
Outputs:
- depth_out: bfloat16 [2048, 8, 1024], P(('ctx', 'tp'))
- grad_query: float32 [2048, 4096], P('ctx', 'tp')
- grad_key: float32 [2048, 4096], P('ctx', 'tp')
- grad_value: float32 [2048, 4096], P('ctx', 'tp')
- grad_proj: float32 [4096, 1024], P('tp', 'ctx')
- grad_gain: float32 [1024], P(('ctx', 'tp'))
The draws below stay inside these ranges and needn't reach their ends.
All inputs are finite; a program needn't handle non-finite values.
Results may differ from the reference program's by a relative error of at most 0.024.
Values may be sent and summed in bfloat16 or wider, within the bound.
No kernel may reach another device: no remote copies, remote signals or barrier semaphores. Data moves between devices by JAX's collectives and lax.ppermute only.
A program may use at most 128 MiB of HBM per device.

```python
import math
import jax
import jax.numpy as jnp
import numpy as np
from jax import lax

HEADS = 32
HEAD_DIM = 128
DEPTH_W = 1024
CODEBOOKS = 8
CARD = 2048
TOK_DEV = 256
DIALOGUES = 4
D = 4096
FRAMES = 2048
N_CTX = 8


def drawn_pair(key):
    folded = jax.random.fold_in(key, 31)
    key_query, key_keys = jax.random.split(folded, 2)
    width_all = HEADS * HEAD_DIM
    query_draw = jnp.clip(jax.random.normal(key_query, (FRAMES, width_all), jnp.float32), -6.0, 6.0)
    key_draw = jnp.clip(jax.random.normal(key_keys, (FRAMES, width_all), jnp.float32), -6.0, 6.0)
    return (query_draw, key_draw)


def draw_queries(key, part):
    return drawn_pair(key)[0].astype(jnp.bfloat16)


def draw_key_rows(key, part):
    return drawn_pair(key)[1].astype(jnp.bfloat16)


def plant(result, key, low, high):
    place = [jax.random.randint(jax.random.fold_in(key, axis), (), 0, length) for axis, length in enumerate(result.shape)]
    main_axis = result.shape.index(max(result.shape))
    neighbour = place[:main_axis] + [(place[main_axis] + 1) % result.shape[main_axis]] + place[main_axis + 1:]
    return result.at[tuple(place)].set(low).at[tuple(neighbour)].set(high)


def spiked(drawn, stream_key, source, target, shards_of, factor):
    owner, partner = [(jnp.arange(drawn.shape[dim]) // (drawn.shape[dim] // shards_of)).reshape([-1 if axis == dim else 1 for axis in range(drawn.ndim)]) for dim in (source, target)]
    chosen = jax.random.permutation(stream_key, shards_of)[partner]
    strong = (owner == chosen) | (owner == (partner + shards_of // 2) % shards_of)
    return jnp.where(strong, factor * drawn, drawn)


def levels(key, shape, cuts, least, largest):
    def one(position, blocks):
        draws = jax.random.uniform(jax.random.fold_in(jax.random.fold_in(key, 6), position), (blocks,), jnp.float32, least / len(cuts), largest / len(cuts))
        return jnp.repeat(jnp.exp(draws), shape[position] // blocks).reshape((-1,) + (1,) * (len(shape) - position - 1))

    level = one(*cuts[0])
    for cut in cuts[1:]:
        level = level * one(*cut)
    return level


def cumulative_ranks(count, skew):
    weights = [(1 << 20) // math.isqrt(standing ** skew) + 1 for standing in range(1, count + 1)]
    width = 1 + sum(weights) // (1 << 30)
    return np.cumsum(np.array([max(1, weight // width) for weight in weights]))


def skewed_ids(own_key, shape, number_of, skew):
    grid = cumulative_ranks(number_of, skew)
    ticket = jax.random.randint(jax.random.fold_in(own_key, 1), shape, 0, int(grid[number_of - 1]))
    standing = jnp.searchsorted(jnp.asarray(grid, jnp.int32), ticket, side="right")
    return jax.random.permutation(jax.random.fold_in(own_key, 2), number_of)[standing].astype(jnp.int32)


def split_up(number_of, total, most, skew):
    portions = [(1 << 20) // math.isqrt(grade ** skew) + 1 for grade in range(2, number_of + 1)]
    spare, counts = total - most - (number_of - 1), [1] * (number_of - 1)
    while spare > 0:
        candidates = [i for i in range(number_of - 1) if counts[i] < most]
        mass, remaining = sum([portions[i] for i in candidates]), spare
        for i in candidates:
            extra = min(most - counts[i], max(1, remaining * portions[i] // mass), spare)
            counts[i] = counts[i] + extra
            spare = spare - extra
    return np.array([most] + counts)


def uneven(key, count, total, limit, slope):
    if count == 2:
        one = jax.random.randint(key, (), max(1, total - limit), min(limit, total - 1) + 1)
        return jnp.stack([one, total - one])
    tallies = jnp.asarray(split_up(count, total, limit, slope), jnp.int32)
    pairs = (count - 1) // 2
    giver, taker = tallies[1:1 + 2 * pairs:2], tallies[2:2 + 2 * pairs:2]
    room = jnp.minimum(giver - 1, limit - taker)
    passed = jax.random.randint(jax.random.fold_in(key, 1), (pairs,), 0, 1 << 20) % (room + 1)
    tallies = tallies.at[1:1 + 2 * pairs:2].set(giver - passed).at[2:2 + 2 * pairs:2].set(taker + passed)
    return tallies[jax.random.permutation(jax.random.fold_in(key, 2), count)]


def scatter_about(stream_key, shape, scale, most, cuts=(), kind=jnp.bfloat16):
    level = levels(stream_key, shape, cuts, -0.22, 0.18) if cuts else 1.0
    result = jax.random.normal(stream_key, shape, jnp.float32) * scale * level
    return jnp.minimum(jnp.maximum(result, -most), most).astype(kind)


def heavy_noise(own_key, dims, spread, limit, shards, heavy, kind=jnp.bfloat16):
    result = spread * jax.random.normal(own_key, dims, jnp.float32)
    if shards:
        result = result * levels(own_key, dims, shards, -0.22, 0.18)
    return jnp.clip(spiked(result, jax.random.fold_in(own_key, 3), *heavy), -limit, limit).astype(kind)


def setup_inputs(seed: int = 0) -> dict:
    keys = jax.random.split(jax.random.key(seed), 10)
    queries = draw_queries(jax.random.fold_in(keys[9], 71), 0)
    key_rows = draw_key_rows(jax.random.fold_in(keys[9], 71), 0)
    value_rows = scatter_about(keys[2], (FRAMES, D), 1.0, 6.0, ((0, 8), (1, 4)))
    segment_ids = jnp.searchsorted(jnp.cumsum(uneven(keys[3], DIALOGUES, FRAMES, FRAMES // 2, 0)), jnp.arange(FRAMES), side="right").astype(jnp.int32)
    codebook_ids = plant(skewed_ids(keys[4], (FRAMES, CODEBOOKS), CARD, 2), jax.random.fold_in(keys[4], 3), 0, CARD - 1).astype(jnp.int32)
    code_table = scatter_about(keys[5], (CODEBOOKS, CARD, DEPTH_W), 0.3, 4.0, ((1, 4),))
    input_proj = scatter_about(keys[6], (D, DEPTH_W), (D // 64) ** -0.5, 0.75)
    norm_gain = jnp.clip(1.0 + 0.18 * jax.random.normal(keys[7], (DEPTH_W,), jnp.float32), 0.1, 1.9)
    upstream = heavy_noise(keys[8], (FRAMES, CODEBOOKS, DEPTH_W), 0.1, 3.0, ((0, 32),), (0, 2, 32, 2.75))
    return {"queries": queries, "key_rows": key_rows, "value_rows": value_rows, "segment_ids": segment_ids, "codebook_ids": codebook_ids, "code_table": code_table, "input_proj": input_proj, "norm_gain": norm_gain, "upstream": upstream}


EPSILON = 1e-06

def split_heads(matrix):
    return matrix.reshape(matrix.shape[0], HEADS, HEAD_DIM).transpose(1, 0, 2)

def merge_heads(stacked):
    return stacked.transpose(1, 0, 2).reshape(stacked.shape[1], HEADS * HEAD_DIM)

def reference(queries, key_rows, value_rows, segment_ids, codebook_ids, code_table, input_proj, norm_gain, upstream):
    score_scale = HEAD_DIM ** (-0.5)
    positions = jnp.arange(FRAMES)
    allowed = (positions[None, :] <= positions[:, None]) & (segment_ids[None, :] == segment_ids[:, None])

    def masked_scores(query_head, key_head):
        scores = jnp.dot(query_head, key_head.T, preferred_element_type=jnp.float32) * score_scale
        return jnp.where(allowed, scores, -jnp.inf)

    def forward_head(inputs):
        query_head, key_head, value_head = inputs
        scores = masked_scores(query_head, key_head)
        top_score = lax.optimization_barrier(jnp.max(scores, axis=1, keepdims=True))
        log_norm = top_score + jnp.log(lax.optimization_barrier(jnp.sum(jnp.exp(scores - top_score), axis=1, keepdims=True)))
        weights = jnp.exp(scores - log_norm).astype(jnp.bfloat16)
        output = jnp.dot(weights, value_head, preferred_element_type=jnp.float32).astype(jnp.bfloat16)
        return (output, log_norm[:, 0])
    query_heads = split_heads(queries)
    key_heads = split_heads(key_rows)
    value_heads = split_heads(value_rows)
    out_heads, log_norms = lax.map(forward_head, (query_heads, key_heads, value_heads))
    attn_out = merge_heads(out_heads)
    projected = jnp.dot(attn_out, input_proj, preferred_element_type=jnp.float32)
    embedded = code_table[jnp.arange(CODEBOOKS)[None, :], codebook_ids]
    hidden = projected[:, None, :] + embedded.astype(jnp.float32)
    inverse = lax.rsqrt(lax.optimization_barrier(jnp.mean(hidden * hidden, axis=2, keepdims=True)) + EPSILON)
    normed = hidden * inverse
    gain_wide = norm_gain.astype(jnp.float32)
    depth_out = (normed * gain_wide).astype(jnp.bfloat16)
    cotangent = upstream.astype(jnp.float32)
    grad_gain = lax.optimization_barrier(jnp.sum(cotangent * normed, axis=(0, 1)))
    grad_normed = cotangent * gain_wide
    grad_hidden = inverse * (grad_normed - normed * lax.optimization_barrier(jnp.mean(grad_normed * normed, axis=2, keepdims=True)))
    grad_sum = lax.optimization_barrier(jnp.sum(grad_hidden, axis=1)).astype(jnp.bfloat16)
    grad_proj = jnp.dot(attn_out.T, grad_sum, preferred_element_type=jnp.float32)
    grad_attn = jnp.dot(grad_sum, input_proj.T, preferred_element_type=jnp.float32).astype(jnp.bfloat16)

    def backward_head(inputs):
        query_head, key_head, value_head, out_head, grad_head, log_norm = inputs
        scores = masked_scores(query_head, key_head)
        probs = jnp.exp(scores - log_norm[:, None])
        weights = probs.astype(jnp.bfloat16)
        row_delta = lax.optimization_barrier(jnp.sum(grad_head.astype(jnp.float32) * out_head.astype(jnp.float32), axis=1, keepdims=True))
        grad_prob = jnp.dot(grad_head, value_head.T, preferred_element_type=jnp.float32)
        grad_score = (probs * (grad_prob - row_delta)).astype(jnp.bfloat16)
        grad_query = jnp.dot(grad_score, key_head, preferred_element_type=jnp.float32) * score_scale
        score_block_list = lax.optimization_barrier(grad_score).astype(jnp.float32).reshape(N_CTX, TOK_DEV, FRAMES)
        weight_block_list = lax.optimization_barrier(weights).astype(jnp.float32).reshape(N_CTX, TOK_DEV, FRAMES)
        query_block_list = query_head.astype(jnp.float32).reshape(N_CTX, TOK_DEV, HEAD_DIM)
        gradient_block_list = grad_head.astype(jnp.float32).reshape(N_CTX, TOK_DEV, HEAD_DIM)
        key_pieces = (jnp.einsum('hru,hrn->hun', score_block_list, query_block_list, precision=lax.Precision.HIGHEST) * score_scale).astype(jnp.bfloat16)
        value_pieces = jnp.einsum('hru,hrn->hun', weight_block_list, gradient_block_list, precision=lax.Precision.HIGHEST).astype(jnp.bfloat16)
        key_sum = lax.optimization_barrier(jnp.sum(lax.optimization_barrier(key_pieces).astype(jnp.float32), axis=0))
        value_sum = lax.optimization_barrier(jnp.sum(lax.optimization_barrier(value_pieces).astype(jnp.float32), axis=0))
        return (grad_query, key_sum, value_sum)
    grad_heads = split_heads(grad_attn)
    query_grads, key_grads, value_grads = lax.map(backward_head, (query_heads, key_heads, value_heads, out_heads, grad_heads, log_norms))
    return (depth_out, merge_heads(query_grads), merge_heads(key_grads), merge_heads(value_grads), grad_proj, grad_gain)
```

```python
import functools

import jax
import jax.numpy as jnp
from jax import lax
from jax.experimental import pallas as pl
from jax.experimental.pallas import tpu as pltpu
from jax.sharding import PartitionSpec as P

HEAD_DIM = 128


NEGATIVE = -1e30
EPSILON = 1e-06
LOG2_E = 1.4426950408889634
SEGMENT_VALUES = 4
VMEM_BYTES = 50 << 20
F32 = jnp.float32
BF16 = jnp.bfloat16


def dot(a, b, a_dim, b_dim):
    return lax.dot_general(a, b, (((a_dim,), (b_dim,)), ((), ())), preferred_element_type=F32)


def call(kernel, name, ids, inputs, out_shapes, scratch=(), in_specs=None, out_specs=None, grid=(1,)):
    def whole(shape):
        return pl.BlockSpec(shape, lambda step, ids: (0,) * len(shape))

    if in_specs is None:
        in_specs = {}
    if out_specs is None:
        out_specs = {}
    return pl.pallas_call(
        kernel,
        name=name,
        out_shape=[jax.ShapeDtypeStruct(shape, dtype) for shape, dtype in out_shapes],
        grid_spec=pltpu.PrefetchScalarGridSpec(
            num_scalar_prefetch=1,
            grid=grid,
            in_specs=[in_specs.get(n, whole(x.shape)) for n, x in enumerate(inputs)],
            out_specs=[out_specs.get(n, whole(shape)) for n, (shape, _) in enumerate(out_shapes)],
            scratch_shapes=list(scratch),
        ),
        compiler_params=pltpu.CompilerParams(vmem_limit_bytes=VMEM_BYTES),
    )(ids, *inputs)


def offset(index, width):
    return pl.multiple_of(index * width, width)


def pack_kernel(n, width, ids, q_ref, k_ref, v_ref, *outs):
    me = ids[0]
    for i in range(n):
        columns = pl.ds(offset(me ^ i, width), width)
        for part, ref in enumerate((q_ref, k_ref, v_ref)):
            outs[i][part] = ref[:, columns]


def segment_starts(seg):
    first = jnp.zeros_like(seg)
    for value in range(SEGMENT_VALUES - 1):
        count = jnp.sum((seg == value).astype(jnp.int32), axis=1, keepdims=True)
        first = first + jnp.where(seg > value, count, 0)
    return first


def visible(starts, low, count, first, rows):
    key_pos = low + lax.broadcasted_iota(jnp.int32, (count, rows), 0)
    query_pos = first + lax.broadcasted_iota(jnp.int32, (count, rows), 1)
    return (key_pos >= starts[:, first : first + rows]) & (key_pos <= query_pos)


def forward_kernel(n, rows, window, factor, ids, seg_ref, *refs):
    pieces, outs = refs[:n], refs[n : 2 * n]
    out_ref, norm_ref, q_s, k_s, v_s = refs[2 * n :]
    me = ids[0]
    for i in range(n):
        place = pl.ds(offset(me ^ i, rows), rows)
        q_s[place, :] = pieces[i][0]
        k_s[place, :] = pieces[i][1]
        v_s[place, :] = pieces[i][2]
    starts = segment_starts(seg_ref[...])
    for block in range(n):
        first, low = block * rows, max(0, block - window) * rows
        count = first + rows - low
        scores = dot(k_s[low : low + count, :], q_s[first : first + rows, :], 1, 1) * factor
        scores = jnp.where(visible(starts, low, count, first, rows), scores, NEGATIVE)
        top = jnp.max(scores, axis=0, keepdims=True)
        mass = jnp.exp2(scores - top)
        total = jnp.sum(mass, axis=0, keepdims=True)
        mixed = dot(v_s[low : low + count, :], mass.astype(BF16), 0, 0) / total
        out_ref[first : first + rows, :] = mixed.T.astype(BF16)
        norm_ref[:, first : first + rows] = top + jnp.log2(total)
    for i in range(n):
        outs[i][...] = out_ref[pl.ds(offset(me ^ i, rows), rows), :]


def backward_kernel(n, rows, window, factor, scale, ids, seg_ref, norm_ref, out_ref, *refs):
    pieces, grads, outs = refs[:n], refs[n : 2 * n], refs[2 * n : 3 * n]
    q_s, k_s, v_s, g_s, dq_s, dk_s, dv_s = refs[3 * n :]
    me = ids[0]
    for i in range(n):
        place = pl.ds(offset(me ^ i, rows), rows)
        q_s[place, :] = pieces[i][0]
        k_s[place, :] = pieces[i][1]
        v_s[place, :] = pieces[i][2]
        g_s[place, :] = grads[i][...]
    starts = segment_starts(seg_ref[...])
    for block in range(n):
        first, low = block * rows, max(0, block - window) * rows
        count = first + rows - low
        keys, query, grad = k_s[low : low + count, :], q_s[first : first + rows, :], g_s[first : first + rows, :]
        scores = dot(keys, query, 1, 1) * factor - norm_ref[:, first : first + rows]
        probs = jnp.exp2(jnp.where(visible(starts, low, count, first, rows), scores, NEGATIVE))
        product = grad.astype(F32) * out_ref[first : first + rows, :].astype(F32)
        delta = jnp.sum(product.T, axis=0, keepdims=True)
        score_grad = (probs * (dot(v_s[low : low + count, :], grad, 1, 1) - delta)).astype(BF16)
        dq_s[first : first + rows, :] = (dot(keys, score_grad, 0, 0).T * scale).astype(BF16)
        key_grad = dot(score_grad, query, 1, 0)
        value_grad = dot(probs.astype(BF16), grad, 1, 0)
        if count > rows:
            dk_s[low:first, :] += key_grad[: count - rows]
            dv_s[low:first, :] += value_grad[: count - rows]
        dk_s[first : first + rows, :] = key_grad[count - rows :]
        dv_s[first : first + rows, :] = value_grad[count - rows :]
    for i in range(n):
        place = pl.ds(offset(me ^ i, rows), rows)
        outs[i][0] = dq_s[place, :]
        outs[i][1] = (dk_s[place, :] * scale).astype(BF16)
        outs[i][2] = dv_s[place, :].astype(BF16)


def project_kernel(n, t, ids, w_ref, *refs):
    pieces, attn_ref, outs, total = refs[:n], refs[n], refs[n + 1 : n + 1 + t], refs[n + 1 + t]
    me, shard = ids[0], ids[1]
    width = pieces[0].shape[1]
    for i in range(n):
        attn_ref[:, pl.ds(offset(me ^ i, width), width)] = pieces[i][...]
    total[...] = dot(attn_ref[...], w_ref[...], 1, 0).astype(BF16)
    rows = outs[0].shape[0]
    for i in range(t):
        outs[i][...] = total[pl.ds(offset(shard ^ i, rows), rows), :]


def lookup_kernel(t, ids, table_ref, *refs):
    codes, outs = refs[:t], refs[t:]
    book = pl.program_id(0)
    shard_rows, rows = table_ref.shape[1], codes[0].shape[0]
    picks = []
    for i in range(t):
        lanes = lax.broadcasted_iota(jnp.int32, codes[i].shape, 1)
        code = jnp.sum(jnp.where(lanes == book, codes[i][...], 0), axis=1, keepdims=True)
        entry = lax.broadcasted_iota(jnp.int32, (rows, shard_rows), 1) + ids[1] * shard_rows
        picks.append((entry == code).astype(F32).astype(BF16))
    found = dot(jnp.concatenate(picks, axis=0), table_ref[0], 1, 0).astype(BF16)
    for i in range(t):
        outs[i][0] = found[i * rows : (i + 1) * rows]


def depth_kernel(t, books, ids, gain_ref, embed_ref, up_ref, *refs):
    parts = refs[:t]
    depth_ref, sum_ref, gain_out_ref = refs[t:]
    projected = parts[0][...].astype(F32)
    for i in range(1, t):
        projected = projected + parts[i][...].astype(F32)
    gain = gain_ref[...]
    grad_sum = jnp.zeros_like(projected)
    gain_sum = jnp.zeros_like(projected)
    for book in range(books):
        hidden = projected + embed_ref[book].astype(F32)
        inverse = lax.rsqrt(jnp.mean(hidden * hidden, axis=1, keepdims=True) + EPSILON)
        normed = hidden * inverse
        depth_ref[book] = (normed * gain).astype(BF16)
        cotangent = up_ref[book].astype(F32)
        gain_sum = gain_sum + cotangent * normed
        grad = cotangent * gain
        grad_sum = grad_sum + inverse * (grad - normed * jnp.mean(grad * normed, axis=1, keepdims=True))
    sum_ref[...] = grad_sum.astype(BF16)
    gain_out_ref[...] = jnp.sum(gain_sum, axis=0, keepdims=True)


def grad_attn_kernel(n, t, ids, w_ref, *refs):
    parts, sum_ref, outs, total = refs[:t], refs[t], refs[t + 1 : t + 1 + n], refs[t + 1 + n]
    me, shard = ids[0], ids[1]
    rows, width = parts[0].shape[0], outs[0].shape[1]
    for i in range(t):
        sum_ref[pl.ds(offset(shard ^ i, rows), rows), :] = parts[i][...]
    total[...] = dot(sum_ref[...], w_ref[...], 1, 1).astype(BF16)
    for i in range(n):
        outs[i][...] = total[:, pl.ds(offset(me ^ i, width), width)]


def grad_proj_kernel(n, ids, attn_ref, sum_ref, send_ref, *refs):
    keeps, total = refs[: n // 2], refs[n // 2]
    me = ids[0]
    width = keeps[0].shape[1]
    total[...] = dot(attn_ref[...], sum_ref[...], 0, 0).astype(BF16)
    for i in range(n // 2):
        mine = me ^ (2 * i)
        keeps[i][...] = total[:, pl.ds(offset(mine, width), width)]
        send_ref[i] = total[:, pl.ds(offset(mine ^ 1, width), width)]


def assemble_kernel(n, ids, *refs):
    pieces, outs = refs[:n], refs[n:]
    me = ids[0]
    width = pieces[0].shape[2]
    for i in range(n):
        columns = pl.ds(offset(me ^ i, width), width)
        for part in range(3):
            outs[part][:, columns] = pieces[i][part].astype(F32)


def swap(x, axis, count, i):
    return lax.ppermute(x, axis, [(b, b ^ i) for b in range(count)])


def swap_all(parts, axis, count):
    return [parts[0]] + [swap(parts[i], axis, count, i) for i in range(1, count)]


def scatter_sum(x, axis, count):
    index = lax.axis_index(axis)
    step = count // 2
    while step:
        half = x.shape[0] // 2
        bit = (index // step) % 2
        kept = lax.dynamic_slice_in_dim(x, bit * half, half, 0)
        sent = lax.dynamic_slice_in_dim(x, (1 - bit) * half, half, 0)
        x = kept + swap(sent, axis, count, step)
        step //= 2
    return x


def heads_body(n, t, queries, key_rows, value_rows, segment_ids, codebook_ids, code_table, input_proj, norm_gain, upstream):
    rows, width = queries.shape
    frames = segment_ids.shape[0]
    books, shard_rows, depth = code_table.shape
    local = codebook_ids.shape[0]
    window = -(-(frames // 2 - 1) // rows)
    scale = HEAD_DIM ** (-0.5)
    factor = scale * LOG2_E
    ids = jnp.stack([lax.axis_index("ctx"), lax.axis_index("tp")]).astype(jnp.int32)
    seg = segment_ids.reshape(1, frames)
    piece = (3, rows, HEAD_DIM)
    tall = (frames, HEAD_DIM)
    w_spec = {0: pl.BlockSpec((width, depth), lambda step, ids: (ids[1], 0))}

    packed = call(
        functools.partial(pack_kernel, n, HEAD_DIM), "pack", ids, [queries, key_rows, value_rows], [(piece, BF16)] * n
    )
    pieces = swap_all(packed, "ctx", n)

    codes = [codebook_ids] + [swap(codebook_ids, "tp", t, i) for i in range(1, t)]
    found = call(
        functools.partial(lookup_kernel, t),
        "lookup",
        ids,
        [code_table] + codes,
        [((books, local, depth), BF16)] * t,
        in_specs={0: pl.BlockSpec((1, shard_rows, depth), lambda step, ids: (step, 0, 0))},
        out_specs={i: pl.BlockSpec((1, local, depth), lambda step, ids: (step, 0, 0)) for i in range(t)},
        grid=(books,),
    )
    embedded = sum(x.astype(F32) for x in swap_all(found, "tp", t)).astype(BF16)
    cotangent = upstream.transpose(1, 0, 2)

    forward = call(
        functools.partial(forward_kernel, n, rows, window, factor),
        "attend",
        ids,
        [seg] + pieces,
        [((rows, HEAD_DIM), BF16)] * n + [(tall, BF16), ((1, frames), F32)],
        [pltpu.VMEM(tall, BF16)] * 3,
    )
    out_pieces, out_full, norm = swap_all(forward[:n], "ctx", n), forward[n], forward[n + 1]
    projected = call(
        functools.partial(project_kernel, n, t),
        "project",
        ids,
        [input_proj] + out_pieces,
        [((rows, width), BF16)] + [((local, depth), BF16)] * t,
        [pltpu.VMEM((rows, depth), BF16)],
        in_specs=w_spec,
    )
    attn_out = projected[0]
    depth_rows, grad_sum, gain_term = call(
        functools.partial(depth_kernel, t, books),
        "depth",
        ids,
        [norm_gain.reshape(1, depth), embedded, cotangent] + swap_all(projected[1:], "tp", t),
        [((books, local, depth), BF16), ((local, depth), BF16), ((1, depth), F32)],
    )
    sums = [grad_sum] + [swap(grad_sum, "tp", t, i) for i in range(1, t)]
    attn_grads = call(
        functools.partial(grad_attn_kernel, n, t),
        "grad_attn",
        ids,
        [input_proj] + sums,
        [((rows, depth), BF16)] + [((rows, HEAD_DIM), BF16)] * n,
        [pltpu.VMEM((rows, width), BF16)],
        in_specs=w_spec,
    )
    grad_pieces = swap_all(attn_grads[1:], "ctx", n)
    slab = (width, depth // n)
    proj_terms = call(
        functools.partial(grad_proj_kernel, n),
        "grad_proj",
        ids,
        [attn_out, attn_grads[0]],
        [((n // 2,) + slab, BF16)] + [(slab, BF16)] * (n // 2),
        [pltpu.VMEM((width, depth), BF16)],
    )
    other = swap(proj_terms[0], "ctx", n, 1)
    pair = [(proj_terms[1 + i].astype(F32) + other[i].astype(F32)) for i in range(n // 2)]
    grad_proj = pair[0]
    for i in range(1, n // 2):
        grad_proj = grad_proj + swap(pair[i].astype(BF16), "ctx", n, 2 * i).astype(F32)

    grads = call(
        functools.partial(backward_kernel, n, rows, window, factor, scale),
        "attend_grad",
        ids,
        [seg, norm, out_full] + pieces + grad_pieces,
        [(piece, BF16)] * n,
        [pltpu.VMEM(tall, BF16)] * 5 + [pltpu.VMEM(tall, F32)] * 2,
    )
    grad_query, grad_key, grad_value = call(
        functools.partial(assemble_kernel, n), "assemble", ids, swap_all(grads, "ctx", n), [((rows, width), F32)] * 3
    )
    gain = scatter_sum(gain_term.reshape(depth), "ctx", n)
    grad_gain = scatter_sum(gain, "tp", t)
    return (depth_rows.transpose(1, 0, 2), grad_query, grad_key, grad_value, grad_proj, grad_gain)


def body(n, t, queries, *rest):
    heads = queries.shape[1] // HEAD_DIM
    if heads == n and n & (n - 1) == 0 and t & (t - 1) == 0 and n > 1:
        return heads_body(n, t, queries, *rest)
    return general_body(queries, *rest)


def general_body(
    queries,
    key_rows,
    value_rows,
    segment_ids,
    codebook_ids,
    code_table,
    input_proj,
    norm_gain,
    upstream,
):
    local_rows = queries.shape[0]
    local_width = queries.shape[1]
    head_count = local_width // HEAD_DIM
    score_scale = HEAD_DIM ** (-0.5)
    ctx_index = lax.axis_index("ctx")
    tp_index = lax.axis_index("tp")
    all_keys, all_values = (
        lax.all_gather(key_rows, "ctx", axis=0, tiled=True),
        lax.all_gather(value_rows, "ctx", axis=0, tiled=True),
    )
    key_total = all_keys.shape[0]
    block_rows = 512
    block_count = key_total // block_rows
    block_list = jnp.arange(block_count, dtype=jnp.int32)
    first_row = ctx_index * local_rows

    def block_scores(query_heads, query_pos, query_seg, block_index):
        key_start = block_index * block_rows
        key_block = lax.dynamic_slice_in_dim(all_keys, key_start, block_rows, 0).reshape(
            block_rows, head_count, HEAD_DIM
        )
        value_block = lax.dynamic_slice_in_dim(all_values, key_start, block_rows, 0).reshape(
            block_rows, head_count, HEAD_DIM
        )
        scores = (
            jnp.einsum("qhd,khd->hqk", query_heads, key_block, preferred_element_type=jnp.float32)
            * score_scale
        )
        key_pos = key_start + jnp.arange(block_rows)
        key_seg = lax.dynamic_slice_in_dim(segment_ids, key_start, block_rows)
        allowed = (key_pos[None, :] <= query_pos[:, None]) & (
            key_seg[None, :] == query_seg[:, None]
        )
        return (jnp.where(allowed[None], scores, NEGATIVE), allowed, key_block, value_block)

    def visit(block_index, last_visible, carried, compute, skipped):
        return lax.cond(block_index * block_rows <= last_visible, compute, skipped, carried)

    def keep_state(state):
        return state

    def describe(query_rows, start_row):
        row_count = query_rows.shape[0]
        query_heads = query_rows.reshape(row_count, head_count, HEAD_DIM)
        query_pos = start_row + jnp.arange(row_count)
        query_seg = lax.dynamic_slice_in_dim(segment_ids, start_row, row_count)
        return (query_heads, query_pos, query_seg, start_row + row_count - 1)

    row_count = queries.shape[0]
    query_heads, query_pos, query_seg, last_visible = describe(queries, first_row)

    def stats_step(carried, block_index):

        def compute(state):
            top_score, row_mass = state
            scores, allowed, key_block, value_block = block_scores(
                query_heads, query_pos, query_seg, block_index
            )
            new_top = jnp.maximum(top_score, jnp.max(scores, axis=2))
            shifted = jnp.where(allowed[None], jnp.exp(scores - new_top[:, :, None]), 0.0)
            return (
                (new_top, row_mass * jnp.exp(top_score - new_top) + jnp.sum(shifted, axis=2)),
                scores,
            )

        def skipped(state):
            return (state, jnp.full((head_count, row_count, block_rows), NEGATIVE, jnp.float32))

        return visit(block_index, last_visible, carried, compute, skipped)

    start_top = jnp.full((head_count, row_count), NEGATIVE, jnp.float32)
    start_mass = jnp.zeros((head_count, row_count), jnp.float32)
    (top_score, row_mass), score_stack = lax.scan(stats_step, (start_top, start_mass), block_list)
    log_norm = top_score + jnp.log(row_mass)

    def output_step(carried, inputs):
        block_index, scores = inputs

        def compute(state):
            key_start = block_index * block_rows
            value_block = lax.dynamic_slice_in_dim(all_values, key_start, block_rows, 0).reshape(
                block_rows, head_count, HEAD_DIM
            )
            weights = jnp.exp(scores - log_norm[:, :, None]).astype(jnp.bfloat16)
            return state + jnp.einsum(
                "hqk,khd->qhd", weights, value_block, preferred_element_type=jnp.float32
            )

        return (visit(block_index, last_visible, carried, compute, keep_state), None)

    start_out = jnp.zeros((row_count, head_count, HEAD_DIM), jnp.float32)
    out_sum, unused = lax.scan(output_step, start_out, (block_list, score_stack))
    group_out = out_sum.reshape(row_count, local_width).astype(jnp.bfloat16)
    attn_out, log_norm = (group_out, log_norm)
    group_codes = lax.all_gather(codebook_ids, "tp", axis=0, tiled=True)
    shard_rows = code_table.shape[1]
    local_codes = group_codes - tp_index * shard_rows
    table_rows = jnp.arange(shard_rows, dtype=jnp.int32)
    selector = (local_codes[:, :, None] == table_rows[None, None, :]).astype(jnp.bfloat16)
    looked = jnp.einsum("tcr,crw->tcw", selector, code_table, preferred_element_type=jnp.float32)
    embedded = lax.psum_scatter(
        looked.astype(jnp.bfloat16), "tp", scatter_dimension=0, tiled=True
    ).astype(jnp.float32)
    w_part = lax.dynamic_slice_in_dim(input_proj, tp_index * local_width, local_width, 0)
    projected = lax.psum_scatter(
        jnp.dot(attn_out, w_part, preferred_element_type=jnp.float32).astype(jnp.bfloat16),
        "tp",
        scatter_dimension=0,
        tiled=True,
    ).astype(jnp.float32)
    hidden = projected[:, None, :] + embedded
    inverse = lax.rsqrt(jnp.mean(hidden * hidden, axis=2, keepdims=True) + EPSILON)
    normed = hidden * inverse
    depth_out = (normed * norm_gain).astype(jnp.bfloat16)
    cotangent = upstream.astype(jnp.float32)
    gain_term = jnp.sum(cotangent * normed, axis=(0, 1))
    grad_gain = lax.psum_scatter(gain_term, ("ctx", "tp"), scatter_dimension=0, tiled=True)
    grad_normed = cotangent * norm_gain
    grad_hidden = inverse * (
        grad_normed - normed * jnp.mean(grad_normed * normed, axis=2, keepdims=True)
    )
    grad_sum = jnp.sum(grad_hidden, axis=1).astype(jnp.bfloat16)
    gathered = lax.all_gather(grad_sum, "tp", axis=0, tiled=True)
    grad_attn = lax.dot_general(
        gathered, w_part, (((1,), (1,)), ((), ())), preferred_element_type=jnp.float32
    ).astype(jnp.bfloat16)
    weight_term = lax.dot_general(
        attn_out, gathered, (((0,), (0,)), ((), ())), preferred_element_type=jnp.float32
    )
    grad_proj = lax.psum_scatter(
        weight_term.astype(jnp.bfloat16), "ctx", scatter_dimension=1, tiled=True
    ).astype(jnp.float32)
    backward_row_count = queries.shape[0]
    backward_query_heads, backward_query_pos, backward_query_seg, backward_last_visible = describe(
        queries, first_row
    )
    grad_heads = grad_attn.reshape(backward_row_count, head_count, HEAD_DIM)
    out_heads = attn_out.reshape(backward_row_count, head_count, HEAD_DIM)
    row_delta = jnp.sum(grad_heads.astype(jnp.float32) * out_heads.astype(jnp.float32), axis=2).T

    def back_step(carried, block_index):

        def compute(query_total):
            scores, allowed, key_block, value_block = block_scores(
                backward_query_heads, backward_query_pos, backward_query_seg, block_index
            )
            probs = jnp.exp(scores - log_norm[:, :, None])
            weights = probs.astype(jnp.bfloat16)
            grad_prob = jnp.einsum(
                "qhd,khd->hqk", grad_heads, value_block, preferred_element_type=jnp.float32
            )
            grad_score = (probs * (grad_prob - row_delta[:, :, None])).astype(jnp.bfloat16)
            query_total = query_total + jnp.einsum(
                "hqk,khd->qhd", grad_score, key_block, preferred_element_type=jnp.float32
            )
            key_grad = (
                jnp.einsum(
                    "hqk,qhd->khd",
                    grad_score,
                    backward_query_heads,
                    preferred_element_type=jnp.float32,
                )
                * score_scale
            )
            value_grad = jnp.einsum(
                "hqk,qhd->khd", weights, grad_heads, preferred_element_type=jnp.float32
            )
            return (
                query_total,
                (
                    key_grad.reshape(block_rows, local_width),
                    value_grad.reshape(block_rows, local_width),
                ),
            )

        def skipped(query_total):
            empty_block = jnp.zeros((block_rows, local_width), jnp.float32)
            return (query_total, (empty_block, empty_block))

        return visit(block_index, backward_last_visible, carried, compute, skipped)

    start_grad = jnp.zeros((backward_row_count, head_count, HEAD_DIM), jnp.float32)
    query_sum, (key_stack, value_stack) = lax.scan(back_step, start_grad, block_list)
    group_query = (query_sum * score_scale).reshape(backward_row_count, local_width)
    key_acc = key_stack.reshape(key_total, local_width)
    value_acc = value_stack.reshape(key_total, local_width)
    grad_key, grad_value = (
        lax.psum_scatter(
            key_acc.astype(jnp.bfloat16), "ctx", scatter_dimension=0, tiled=True
        ).astype(jnp.float32),
        lax.psum_scatter(
            value_acc.astype(jnp.bfloat16), "ctx", scatter_dimension=0, tiled=True
        ).astype(jnp.float32),
    )
    return (depth_out, group_query, grad_key, grad_value, grad_proj, grad_gain)


def solution(mesh):
    return jax.shard_map(
        functools.partial(body, mesh.shape["ctx"], mesh.shape["tp"]),
        mesh=mesh,
        in_specs=(
            P("ctx", "tp"),
            P("ctx", "tp"),
            P("ctx", "tp"),
            P(),
            P(("ctx", "tp"), None),
            P(None, "tp", None),
            P(),
            P(),
            P(("ctx", "tp"), None, None),
        ),
        out_specs=(
            P(("ctx", "tp"), None, None),
            P("ctx", "tp"),
            P("ctx", "tp"),
            P("ctx", "tp"),
            P("tp", "ctx"),
            P(("ctx", "tp")),
        ),
        check_vma=False,
    )
```

```python
import functools
import math

import jax
import jax.numpy as jnp
from jax import lax
from jax.experimental import pallas as pl
from jax.experimental.pallas import tpu as pltpu
from jax.sharding import PartitionSpec as P

HEAD_DIM = 128


NEGATIVE = -1e30
EPSILON = 1e-06
LOG2_E = 1.4426950408889634
SEGMENT_VALUES = 4
VMEM_BYTES = 50 << 20
F32 = jnp.float32
BF16 = jnp.bfloat16


def dot(a, b, a_dim, b_dim):
    return lax.dot_general(a, b, (((a_dim,), (b_dim,)), ((), ())), preferred_element_type=F32)


def call(kernel, name, ids, inputs, out_shapes, scratch=(), in_specs=None, out_specs=None, grid=(1,), flops=0, extra=0, skip=0):
    def whole(shape):
        return pl.BlockSpec(shape, lambda step, ids: (0,) * len(shape))

    if in_specs is None:
        in_specs = {}
    if out_specs is None:
        out_specs = {}
    return pl.pallas_call(
        kernel,
        name=name,
        out_shape=[jax.ShapeDtypeStruct(shape, dtype) for shape, dtype in out_shapes],
        grid_spec=pltpu.PrefetchScalarGridSpec(
            num_scalar_prefetch=1,
            grid=grid,
            in_specs=[in_specs.get(n, whole(x.shape)) for n, x in enumerate(inputs)],
            out_specs=[out_specs.get(n, whole(shape)) for n, (shape, _) in enumerate(out_shapes)],
            scratch_shapes=list(scratch),
        ),
        compiler_params=pltpu.CompilerParams(vmem_limit_bytes=VMEM_BYTES),
        cost_estimate=pl.CostEstimate(
            flops=flops,
            transcendentals=0,
            bytes_accessed=extra + sum(x.size * x.dtype.itemsize for x in inputs[skip:]) + sum(math.prod(o[0]) * 2 for o in out_shapes),
        ),
    )(ids, *inputs)


def offset(index, width):
    return pl.multiple_of(index * width, width)


def pack_kernel(n, width, ids, q_ref, k_ref, v_ref, *refs):
    outs, sem = refs[:n], refs[n]
    me = ids[0]
    copies = []
    for i in range(n):
        columns = pl.ds(offset(me ^ i, width), width)
        for part, ref in enumerate((q_ref, k_ref, v_ref)):
            copies.append(pltpu.make_async_copy(ref.at[:, columns], outs[i].at[part], sem.at[3 * i + part]))
            copies[-1].start()
    for copy in copies:
        copy.wait()


def segment_starts(seg):
    first = jnp.zeros_like(seg)
    for value in range(SEGMENT_VALUES - 1):
        count = jnp.sum((seg == value).astype(jnp.int32), axis=1, keepdims=True)
        first = first + jnp.where(seg > value, count, 0)
    return first


def visible(starts, low, count, first, rows):
    key_pos = low + lax.broadcasted_iota(jnp.int32, (count, rows), 0)
    query_pos = first + lax.broadcasted_iota(jnp.int32, (count, rows), 1)
    return (key_pos >= starts[:, first : first + rows]) & (key_pos <= query_pos)


def forward_kernel(n, rows, window, factor, ids, seg_ref, *refs):
    pieces = refs[:n]
    out_ref, norm_ref, q_s, k_s, v_s = refs[n:]
    me = ids[0]
    for i in range(n):
        place = pl.ds(offset(me ^ i, rows), rows)
        q_s[place, :] = pieces[i][0]
        k_s[place, :] = pieces[i][1]
        v_s[place, :] = pieces[i][2]
    starts = segment_starts(seg_ref[...])
    for block in range(n):
        first, low = block * rows, max(0, block - window) * rows
        count = first + rows - low
        scores = dot(k_s[low : low + count, :], q_s[first : first + rows, :], 1, 1) * factor
        scores = jnp.where(visible(starts, low, count, first, rows), scores, NEGATIVE)
        top = jnp.max(scores, axis=0, keepdims=True)
        mass = jnp.exp2(scores - top)
        total = jnp.sum(mass, axis=0, keepdims=True)
        mixed = dot(v_s[low : low + count, :], mass.astype(BF16), 0, 0) / total
        out_ref[first : first + rows, :] = mixed.T.astype(BF16)
        norm_ref[:, first : first + rows] = top + jnp.log2(total)


def backward_kernel(n, rows, window, factor, scale, ids, seg_ref, norm_ref, out_ref, q_s, k_s, v_s, g_s, *refs):
    outs = refs[:n]
    dq_s, dk_s, dv_s = refs[n:]
    me = ids[0]
    starts = segment_starts(seg_ref[...])
    for block in range(n):
        first, low = block * rows, max(0, block - window) * rows
        count = first + rows - low
        keys, query, grad = k_s[low : low + count, :], q_s[first : first + rows, :], g_s[first : first + rows, :]
        scores = dot(keys, query, 1, 1) * factor - norm_ref[:, first : first + rows]
        probs = jnp.exp2(jnp.where(visible(starts, low, count, first, rows), scores, NEGATIVE))
        product = grad.astype(F32) * out_ref[first : first + rows, :].astype(F32)
        delta = jnp.sum(product.T, axis=0, keepdims=True)
        score_grad = (probs * (dot(v_s[low : low + count, :], grad, 1, 1) - delta)).astype(BF16)
        dq_s[first : first + rows, :] = (dot(keys, score_grad, 0, 0).T * scale).astype(BF16)
        key_grad = dot(score_grad, query, 1, 0)
        value_grad = dot(probs.astype(BF16), grad, 1, 0)
        if count > rows:
            dk_s[low:first, :] += key_grad[: count - rows]
            dv_s[low:first, :] += value_grad[: count - rows]
        dk_s[first : first + rows, :] = key_grad[count - rows :]
        dv_s[first : first + rows, :] = value_grad[count - rows :]
    for i in range(n):
        place = pl.ds(offset(me ^ i, rows), rows)
        outs[i][0] = dq_s[place, :]
        outs[i][1] = (dk_s[place, :] * scale).astype(BF16)
        outs[i][2] = dv_s[place, :].astype(BF16)


def project_kernel(n, t, ids, w_ref, heads_ref, *refs):
    attn_ref, outs, total = refs[0], refs[1 : 1 + t], refs[1 + t]
    shard = ids[1]
    for i in range(n):
        attn_ref[:, i * HEAD_DIM : (i + 1) * HEAD_DIM] = heads_ref[i]
    total[...] = dot(attn_ref[...], w_ref[...], 1, 0).astype(BF16)
    rows = outs[0].shape[0]
    for i in range(t):
        outs[i][...] = total[pl.ds(offset(shard ^ i, rows), rows), :]


def lookup_kernel(t, ids, table_ref, *refs):
    codes, outs = refs[:t], refs[t:]
    book = pl.program_id(0)
    shard_rows, rows = table_ref.shape[1], codes[0].shape[0]
    picks = []
    for i in range(t):
        lanes = lax.broadcasted_iota(jnp.int32, codes[i].shape, 1)
        code = jnp.sum(jnp.where(lanes == book, codes[i][...], 0), axis=1, keepdims=True)
        entry = lax.broadcasted_iota(jnp.int32, (rows, shard_rows), 1) + ids[1] * shard_rows
        picks.append((entry == code).astype(F32).astype(BF16))
    found = dot(jnp.concatenate(picks, axis=0), table_ref[0], 1, 0).astype(BF16)
    for i in range(t):
        outs[i][0] = found[i * rows : (i + 1) * rows]


def depth_kernel(t, books, ids, gain_ref, embed_ref, up_ref, *refs):
    parts = refs[:t]
    depth_ref, sum_ref = refs[t:]
    projected = parts[0][...].astype(F32)
    for i in range(1, t):
        projected = projected + parts[i][...].astype(F32)
    gain = gain_ref[...]
    grad_sum = jnp.zeros_like(projected)
    gain_sum = jnp.zeros_like(projected)
    for book in range(books):
        hidden = projected + embed_ref[book].astype(F32)
        inverse = lax.rsqrt(jnp.mean(hidden * hidden, axis=1, keepdims=True) + EPSILON)
        normed = hidden * inverse
        depth_ref[book] = (normed * gain).astype(BF16)
        cotangent = up_ref[book].astype(F32)
        gain_sum = gain_sum + cotangent * normed
        grad = cotangent * gain
        grad_sum = grad_sum + inverse * (grad - normed * jnp.mean(grad * normed, axis=1, keepdims=True))
    rows = grad_sum.shape[0]
    sum_ref[:rows, :] = grad_sum.astype(BF16)
    sum_ref[rows:, :] = two_parts(jnp.sum(gain_sum, axis=0, keepdims=True), 0, sum_ref.shape[0] - rows)


def two_parts(row, slot, count):
    high = row.astype(BF16).astype(F32)
    place = lax.broadcasted_iota(jnp.int32, (count, row.shape[1]), 0)
    return jnp.where(place == 2 * slot, high, jnp.where(place == 2 * slot + 1, row - high, 0.0)).astype(BF16)


def grad_attn_kernel(n, t, ids, w_ref, attn_ref, *refs):
    parts, out_ref, proj_ref, sum_s = refs[:t], refs[t], refs[t + 1], refs[t + 2]
    me, shard = ids[0], ids[1]
    rows = sum_s.shape[0] // t
    gain = jnp.zeros((1, sum_s.shape[1]), F32)
    for i in range(t):
        sum_s[pl.ds(offset(shard ^ i, rows), rows), :] = parts[i][:rows, :]
        gain = gain + jnp.sum(parts[i][rows:, :].astype(F32), axis=0, keepdims=True)
    grad = dot(sum_s[...], w_ref[...], 1, 1).astype(BF16)
    for i in range(n):
        out_ref[i] = grad[:, i * HEAD_DIM : (i + 1) * HEAD_DIM]
    term = dot(attn_ref[...], sum_s[...], 0, 0).astype(BF16)
    tail = two_parts(gain, me, 2 * n)
    width, columns = term.shape[0], proj_ref.shape[2]
    for i in range(n):
        proj_ref[i, :width, :] = term[:, i * columns : (i + 1) * columns]
        proj_ref[i, width:, :] = tail[:, i * columns : (i + 1) * columns]


def assemble_kernel(n, ids, *refs):
    pieces, outs = refs[:n], refs[n:]
    me = ids[0]
    width = pieces[0].shape[2]
    for i in range(n):
        columns = pl.ds(offset(me ^ i, width), width)
        for part in range(3):
            outs[part][:, columns] = pieces[i][part].astype(F32)


def swap(x, axis, count, i):
    return lax.ppermute(x, axis, [(b, b ^ i) for b in range(count)])


def swap_all(parts, axis, count):
    return [parts[0]] + [swap(parts[i], axis, count, i) for i in range(1, count)]


def heads_body(n, t, queries, key_rows, value_rows, segment_ids, codebook_ids, code_table, input_proj, norm_gain, upstream):
    rows, width = queries.shape
    frames = segment_ids.shape[0]
    books, shard_rows, depth = code_table.shape
    local = codebook_ids.shape[0]
    window = -(-(frames // 2 - 1) // rows)
    scale = HEAD_DIM ** (-0.5)
    factor = scale * LOG2_E
    ids = jnp.stack([lax.axis_index("ctx"), lax.axis_index("tp")]).astype(jnp.int32)
    seg = segment_ids.reshape(1, frames)
    piece = (3, rows, HEAD_DIM)
    tall = (frames, HEAD_DIM)
    w_spec = {0: pl.BlockSpec((width, depth), lambda step, ids: (ids[1], 0))}

    raw = pl.BlockSpec(memory_space=pl.ANY)
    packed = call(
        functools.partial(pack_kernel, n, HEAD_DIM),
        "pack",
        ids,
        [queries, key_rows, value_rows],
        [(piece, BF16)] * n,
        [pltpu.SemaphoreType.DMA((3 * n,))],
        in_specs={i: raw for i in range(3)},
        out_specs={i: raw for i in range(n)},
    )
    pieces = swap_all(packed, "ctx", n)

    codes = [codebook_ids] + [swap(codebook_ids, "tp", t, i) for i in range(1, t)]
    found = call(
        functools.partial(lookup_kernel, t),
        "lookup",
        ids,
        [code_table] + codes,
        [((books, local, depth), BF16)] * t,
        in_specs={0: pl.BlockSpec((1, shard_rows, depth), lambda step, ids: (step, 0, 0))},
        out_specs={i: pl.BlockSpec((1, local, depth), lambda step, ids: (step, 0, 0)) for i in range(t)},
        grid=(books,),
        flops=2 * books * t * local * shard_rows * depth,
    )
    embedded = sum(x.astype(F32) for x in swap_all(found, "tp", t)).astype(BF16)
    cotangent = upstream.transpose(1, 0, 2)

    pair_flops = 4 * frames * (window + 1) * rows * HEAD_DIM
    out_full, norm, query, key, value = call(
        functools.partial(forward_kernel, n, rows, window, factor),
        "attend",
        ids,
        [seg] + pieces,
        [(tall, BF16), ((1, frames), F32)] + [(tall, BF16)] * 3,
        flops=pair_flops,
    )
    out_heads = lax.all_to_all(out_full.reshape(n, rows, HEAD_DIM), "ctx", 0, 0, tiled=True)
    projected = call(
        functools.partial(project_kernel, n, t),
        "project",
        ids,
        [input_proj, out_heads],
        [((rows, width), BF16)] + [((local, depth), BF16)] * t,
        [pltpu.VMEM((rows, depth), BF16)],
        in_specs=w_spec,
        flops=2 * rows * width * depth,
        extra=2 * width * depth,
        skip=1,
    )
    attn_out = projected[0]
    extra_rows = 16
    depth_rows, grad_sum = call(
        functools.partial(depth_kernel, t, books),
        "depth",
        ids,
        [norm_gain.reshape(1, depth), embedded, cotangent] + swap_all(projected[1:], "tp", t),
        [((books, local, depth), BF16), ((local + extra_rows, depth), BF16)],
    )
    sums = [grad_sum] + [swap(grad_sum, "tp", t, i) for i in range(1, t)]
    grad_heads, proj_term = call(
        functools.partial(grad_attn_kernel, n, t),
        "grad_attn",
        ids,
        [input_proj, attn_out] + sums,
        [((n, rows, HEAD_DIM), BF16), ((n, width + 2 * n, depth // n), BF16)],
        [pltpu.VMEM((rows, depth), BF16)],
        in_specs=w_spec,
        flops=4 * rows * width * depth,
        extra=2 * width * depth,
        skip=1,
    )
    proj_sum = lax.psum_scatter(
        proj_term.reshape(n * (width + 2 * n), depth // n), "ctx", scatter_dimension=0, tiled=True
    )
    grad_full = lax.all_to_all(grad_heads, "ctx", 0, 0, tiled=True).reshape(tall)
    grads = call(
        functools.partial(backward_kernel, n, rows, window, factor, scale),
        "attend_grad",
        ids,
        [seg, norm, out_full, query, key, value, grad_full],
        [(piece, BF16)] * n,
        [pltpu.VMEM(tall, BF16)] + [pltpu.VMEM(tall, F32)] * 2,
        flops=5 * pair_flops // 2,
    )
    grad_query, grad_key, grad_value = call(
        functools.partial(assemble_kernel, n), "assemble", ids, swap_all(grads, "ctx", n), [((rows, width), F32)] * 3
    )
    grad_proj = proj_sum[:width].astype(F32)
    gain = jnp.sum(proj_sum[width:].astype(F32), axis=0)
    part = depth // (n * t)
    grad_gain = lax.dynamic_slice_in_dim(gain, lax.axis_index("tp") * part, part, 0)
    return (depth_rows.transpose(1, 0, 2), grad_query, grad_key, grad_value, grad_proj, grad_gain)


def body(n, t, queries, *rest):
    heads = queries.shape[1] // HEAD_DIM
    if heads == n and n & (n - 1) == 0 and t & (t - 1) == 0 and n > 1:
        return heads_body(n, t, queries, *rest)
    return general_body(queries, *rest)


def general_body(
    queries,
    key_rows,
    value_rows,
    segment_ids,
    codebook_ids,
    code_table,
    input_proj,
    norm_gain,
    upstream,
):
    local_rows = queries.shape[0]
    local_width = queries.shape[1]
    head_count = local_width // HEAD_DIM
    score_scale = HEAD_DIM ** (-0.5)
    ctx_index = lax.axis_index("ctx")
    tp_index = lax.axis_index("tp")
    all_keys, all_values = (
        lax.all_gather(key_rows, "ctx", axis=0, tiled=True),
        lax.all_gather(value_rows, "ctx", axis=0, tiled=True),
    )
    key_total = all_keys.shape[0]
    block_rows = 512
    block_count = key_total // block_rows
    block_list = jnp.arange(block_count, dtype=jnp.int32)
    first_row = ctx_index * local_rows

    def block_scores(query_heads, query_pos, query_seg, block_index):
        key_start = block_index * block_rows
        key_block = lax.dynamic_slice_in_dim(all_keys, key_start, block_rows, 0).reshape(
            block_rows, head_count, HEAD_DIM
        )
        value_block = lax.dynamic_slice_in_dim(all_values, key_start, block_rows, 0).reshape(
            block_rows, head_count, HEAD_DIM
        )
        scores = (
            jnp.einsum("qhd,khd->hqk", query_heads, key_block, preferred_element_type=jnp.float32)
            * score_scale
        )
        key_pos = key_start + jnp.arange(block_rows)
        key_seg = lax.dynamic_slice_in_dim(segment_ids, key_start, block_rows)
        allowed = (key_pos[None, :] <= query_pos[:, None]) & (
            key_seg[None, :] == query_seg[:, None]
        )
        return (jnp.where(allowed[None], scores, NEGATIVE), allowed, key_block, value_block)

    def visit(block_index, last_visible, carried, compute, skipped):
        return lax.cond(block_index * block_rows <= last_visible, compute, skipped, carried)

    def keep_state(state):
        return state

    def describe(query_rows, start_row):
        row_count = query_rows.shape[0]
        query_heads = query_rows.reshape(row_count, head_count, HEAD_DIM)
        query_pos = start_row + jnp.arange(row_count)
        query_seg = lax.dynamic_slice_in_dim(segment_ids, start_row, row_count)
        return (query_heads, query_pos, query_seg, start_row + row_count - 1)

    row_count = queries.shape[0]
    query_heads, query_pos, query_seg, last_visible = describe(queries, first_row)

    def stats_step(carried, block_index):

        def compute(state):
            top_score, row_mass = state
            scores, allowed, key_block, value_block = block_scores(
                query_heads, query_pos, query_seg, block_index
            )
            new_top = jnp.maximum(top_score, jnp.max(scores, axis=2))
            shifted = jnp.where(allowed[None], jnp.exp(scores - new_top[:, :, None]), 0.0)
            return (
                (new_top, row_mass * jnp.exp(top_score - new_top) + jnp.sum(shifted, axis=2)),
                scores,
            )

        def skipped(state):
            return (state, jnp.full((head_count, row_count, block_rows), NEGATIVE, jnp.float32))

        return visit(block_index, last_visible, carried, compute, skipped)

    start_top = jnp.full((head_count, row_count), NEGATIVE, jnp.float32)
    start_mass = jnp.zeros((head_count, row_count), jnp.float32)
    (top_score, row_mass), score_stack = lax.scan(stats_step, (start_top, start_mass), block_list)
    log_norm = top_score + jnp.log(row_mass)

    def output_step(carried, inputs):
        block_index, scores = inputs

        def compute(state):
            key_start = block_index * block_rows
            value_block = lax.dynamic_slice_in_dim(all_values, key_start, block_rows, 0).reshape(
                block_rows, head_count, HEAD_DIM
            )
            weights = jnp.exp(scores - log_norm[:, :, None]).astype(jnp.bfloat16)
            return state + jnp.einsum(
                "hqk,khd->qhd", weights, value_block, preferred_element_type=jnp.float32
            )

        return (visit(block_index, last_visible, carried, compute, keep_state), None)

    start_out = jnp.zeros((row_count, head_count, HEAD_DIM), jnp.float32)
    out_sum, unused = lax.scan(output_step, start_out, (block_list, score_stack))
    group_out = out_sum.reshape(row_count, local_width).astype(jnp.bfloat16)
    attn_out, log_norm = (group_out, log_norm)
    group_codes = lax.all_gather(codebook_ids, "tp", axis=0, tiled=True)
    shard_rows = code_table.shape[1]
    local_codes = group_codes - tp_index * shard_rows
    table_rows = jnp.arange(shard_rows, dtype=jnp.int32)
    selector = (local_codes[:, :, None] == table_rows[None, None, :]).astype(jnp.bfloat16)
    looked = jnp.einsum("tcr,crw->tcw", selector, code_table, preferred_element_type=jnp.float32)
    embedded = lax.psum_scatter(
        looked.astype(jnp.bfloat16), "tp", scatter_dimension=0, tiled=True
    ).astype(jnp.float32)
    w_part = lax.dynamic_slice_in_dim(input_proj, tp_index * local_width, local_width, 0)
    projected = lax.psum_scatter(
        jnp.dot(attn_out, w_part, preferred_element_type=jnp.float32).astype(jnp.bfloat16),
        "tp",
        scatter_dimension=0,
        tiled=True,
    ).astype(jnp.float32)
    hidden = projected[:, None, :] + embedded
    inverse = lax.rsqrt(jnp.mean(hidden * hidden, axis=2, keepdims=True) + EPSILON)
    normed = hidden * inverse
    depth_out = (normed * norm_gain).astype(jnp.bfloat16)
    cotangent = upstream.astype(jnp.float32)
    gain_term = jnp.sum(cotangent * normed, axis=(0, 1))
    grad_gain = lax.psum_scatter(gain_term, ("ctx", "tp"), scatter_dimension=0, tiled=True)
    grad_normed = cotangent * norm_gain
    grad_hidden = inverse * (
        grad_normed - normed * jnp.mean(grad_normed * normed, axis=2, keepdims=True)
    )
    grad_sum = jnp.sum(grad_hidden, axis=1).astype(jnp.bfloat16)
    gathered = lax.all_gather(grad_sum, "tp", axis=0, tiled=True)
    grad_attn = lax.dot_general(
        gathered, w_part, (((1,), (1,)), ((), ())), preferred_element_type=jnp.float32
    ).astype(jnp.bfloat16)
    weight_term = lax.dot_general(
        attn_out, gathered, (((0,), (0,)), ((), ())), preferred_element_type=jnp.float32
    )
    grad_proj = lax.psum_scatter(
        weight_term.astype(jnp.bfloat16), "ctx", scatter_dimension=1, tiled=True
    ).astype(jnp.float32)
    backward_row_count = queries.shape[0]
    backward_query_heads, backward_query_pos, backward_query_seg, backward_last_visible = describe(
        queries, first_row
    )
    grad_heads = grad_attn.reshape(backward_row_count, head_count, HEAD_DIM)
    out_heads = attn_out.reshape(backward_row_count, head_count, HEAD_DIM)
    row_delta = jnp.sum(grad_heads.astype(jnp.float32) * out_heads.astype(jnp.float32), axis=2).T

    def back_step(carried, block_index):

        def compute(query_total):
            scores, allowed, key_block, value_block = block_scores(
                backward_query_heads, backward_query_pos, backward_query_seg, block_index
            )
            probs = jnp.exp(scores - log_norm[:, :, None])
            weights = probs.astype(jnp.bfloat16)
            grad_prob = jnp.einsum(
                "qhd,khd->hqk", grad_heads, value_block, preferred_element_type=jnp.float32
            )
            grad_score = (probs * (grad_prob - row_delta[:, :, None])).astype(jnp.bfloat16)
            query_total = query_total + jnp.einsum(
                "hqk,khd->qhd", grad_score, key_block, preferred_element_type=jnp.float32
            )
            key_grad = (
                jnp.einsum(
                    "hqk,qhd->khd",
                    grad_score,
                    backward_query_heads,
                    preferred_element_type=jnp.float32,
                )
                * score_scale
            )
            value_grad = jnp.einsum(
                "hqk,qhd->khd", weights, grad_heads, preferred_element_type=jnp.float32
            )
            return (
                query_total,
                (
                    key_grad.reshape(block_rows, local_width),
                    value_grad.reshape(block_rows, local_width),
                ),
            )

        def skipped(query_total):
            empty_block = jnp.zeros((block_rows, local_width), jnp.float32)
            return (query_total, (empty_block, empty_block))

        return visit(block_index, backward_last_visible, carried, compute, skipped)

    start_grad = jnp.zeros((backward_row_count, head_count, HEAD_DIM), jnp.float32)
    query_sum, (key_stack, value_stack) = lax.scan(back_step, start_grad, block_list)
    group_query = (query_sum * score_scale).reshape(backward_row_count, local_width)
    key_acc = key_stack.reshape(key_total, local_width)
    value_acc = value_stack.reshape(key_total, local_width)
    grad_key, grad_value = (
        lax.psum_scatter(
            key_acc.astype(jnp.bfloat16), "ctx", scatter_dimension=0, tiled=True
        ).astype(jnp.float32),
        lax.psum_scatter(
            value_acc.astype(jnp.bfloat16), "ctx", scatter_dimension=0, tiled=True
        ).astype(jnp.float32),
    )
    return (depth_out, group_query, grad_key, grad_value, grad_proj, grad_gain)


def solution(mesh):
    return jax.shard_map(
        functools.partial(body, mesh.shape["ctx"], mesh.shape["tp"]),
        mesh=mesh,
        in_specs=(
            P("ctx", "tp"),
            P("ctx", "tp"),
            P("ctx", "tp"),
            P(),
            P(("ctx", "tp"), None),
            P(None, "tp", None),
            P(),
            P(),
            P(("ctx", "tp"), None, None),
        ),
        out_specs=(
            P(("ctx", "tp"), None, None),
            P("ctx", "tp"),
            P("ctx", "tp"),
            P("ctx", "tp"),
            P("tp", "ctx"),
            P(("ctx", "tp")),
        ),
        check_vma=False,
    )
```

```python
import functools
import math

import jax
import jax.numpy as jnp
from jax import lax
from jax.experimental import pallas as pl
from jax.experimental.pallas import tpu as pltpu
from jax.sharding import PartitionSpec as P

HEAD_DIM = 128


NEGATIVE = -1e30
EPSILON = 1e-06
LOG2_E = 1.4426950408889634
SEGMENT_VALUES = 4
GAIN_SLOTS = 8
MIB = 1 << 20
F32 = jnp.float32
BF16 = jnp.bfloat16


def dot(a, b, a_dim, b_dim):
    return lax.dot_general(a, b, (((a_dim,), (b_dim,)), ((), ())), preferred_element_type=F32)


def call(kernel, name, ids, inputs, out_shapes, scratch=(), in_specs=None, out_specs=None, grid=(1,), flops=0, vmem=16, costly=True):
    def whole(shape):
        return pl.BlockSpec(shape, lambda step, ids: (0,) * len(shape))

    if in_specs is None:
        in_specs = {}
    if out_specs is None:
        out_specs = {}
    return pl.pallas_call(
        kernel,
        name=name,
        out_shape=[jax.ShapeDtypeStruct(shape, dtype) for shape, dtype in out_shapes],
        grid_spec=pltpu.PrefetchScalarGridSpec(
            num_scalar_prefetch=1,
            grid=grid,
            in_specs=[in_specs.get(n, whole(x.shape)) for n, x in enumerate(inputs)],
            out_specs=[out_specs.get(n, whole(shape)) for n, (shape, _) in enumerate(out_shapes)],
            scratch_shapes=list(scratch),
        ),
        compiler_params=pltpu.CompilerParams(vmem_limit_bytes=vmem * MIB),
        cost_estimate=pl.CostEstimate(
            flops=flops,
            transcendentals=0,
            bytes_accessed=0 if not costly else sum(x.size * x.dtype.itemsize for x in inputs) + sum(math.prod(o[0]) * 2 for o in out_shapes),
        ),
    )(ids, *inputs)


def offset(index, width):
    return pl.multiple_of(index * width, width)


def pack_kernel(n, ids, q_ref, k_ref, v_ref, out_ref, sem):
    copies = []
    for part, ref in enumerate((q_ref, k_ref, v_ref)):
        for i in range(n):
            columns = ref.at[:, i * HEAD_DIM : (i + 1) * HEAD_DIM]
            copies.append(pltpu.make_async_copy(columns, out_ref.at[i, part], sem.at[part * n + i]))
            copies[-1].start()
    for copy in copies:
        copy.wait()


def segment_starts(seg):
    first = jnp.zeros_like(seg)
    for value in range(SEGMENT_VALUES - 1):
        count = jnp.sum((seg == value).astype(jnp.int32), axis=1, keepdims=True)
        first = first + jnp.where(seg > value, count, 0)
    return first


def visible(starts, low, count, first, rows):
    key_pos = low + lax.broadcasted_iota(jnp.int32, (count, rows), 0)
    query_pos = first + lax.broadcasted_iota(jnp.int32, (count, rows), 1)
    return (key_pos >= starts[:, first : first + rows]) & (key_pos <= query_pos)


def rows_of(pieces_ref, part, low, high):
    return jnp.concatenate([pieces_ref[i, part] for i in range(low, high)], axis=0)


def forward_kernel(n, rows, window, factor, ids, seg_ref, pieces_ref, out_ref, norm_ref):
    starts = segment_starts(seg_ref[...])
    for block in range(n):
        first, low = block * rows, max(0, block - window) * rows
        count = first + rows - low
        keys = rows_of(pieces_ref, 1, low // rows, block + 1)
        values = rows_of(pieces_ref, 2, low // rows, block + 1)
        scores = dot(keys, pieces_ref[block, 0], 1, 1) * factor
        scores = jnp.where(visible(starts, low, count, first, rows), scores, NEGATIVE)
        top = jnp.max(scores, axis=0, keepdims=True)
        mass = jnp.exp2(scores - top)
        total = jnp.sum(mass, axis=0, keepdims=True)
        mixed = dot(values, mass.astype(BF16), 0, 0) / total
        out_ref[first : first + rows, :] = mixed.T.astype(BF16)
        norm_ref[:, first : first + rows] = top + jnp.log2(total)


def probs_kernel(n, rows, window, factor, ids, seg_ref, norm_ref, pieces_ref, probs_ref):
    starts = segment_starts(seg_ref[...])
    place = 0
    for block in range(n):
        first, low = block * rows, max(0, block - window) * rows
        count = first + rows - low
        keys = rows_of(pieces_ref, 1, low // rows, block + 1)
        scores = dot(keys, pieces_ref[block, 0], 1, 1) * factor - norm_ref[:, first : first + rows]
        probs = jnp.exp2(jnp.where(visible(starts, low, count, first, rows), scores, NEGATIVE))
        probs_ref[place : place + count, :] = probs.astype(BF16)
        place += count


def backward_kernel(n, rows, window, scale, ids, probs_ref, out_ref, pieces_ref, g_s, grads_ref, dk_s, dv_s):
    place = 0
    for block in range(n):
        first, low = block * rows, max(0, block - window) * rows
        count = first + rows - low
        keys = rows_of(pieces_ref, 1, low // rows, block + 1)
        values = rows_of(pieces_ref, 2, low // rows, block + 1)
        query, grad = pieces_ref[block, 0], g_s[first : first + rows, :]
        probs = probs_ref[place : place + count, :]
        place += count
        product = grad.astype(F32) * out_ref[first : first + rows, :].astype(F32)
        delta = jnp.sum(product.T, axis=0, keepdims=True)
        score_grad = (probs.astype(F32) * (dot(values, grad, 1, 1) - delta)).astype(BF16)
        grads_ref[block, 0] = (dot(keys, score_grad, 0, 0).T * scale).astype(BF16)
        key_grad = dot(score_grad, query, 1, 0)
        value_grad = dot(probs, grad, 1, 0)
        if count > rows:
            dk_s[low:first, :] += key_grad[: count - rows]
            dv_s[low:first, :] += value_grad[: count - rows]
        dk_s[first : first + rows, :] = key_grad[count - rows :]
        dv_s[first : first + rows, :] = value_grad[count - rows :]
    for i in range(n):
        grads_ref[i, 1] = (dk_s[i * rows : (i + 1) * rows, :] * scale).astype(BF16)
        grads_ref[i, 2] = dv_s[i * rows : (i + 1) * rows, :].astype(BF16)


def project_kernel(n, t, ids, w_ref, heads_ref, *refs):
    attn_ref, outs, total = refs[0], refs[1 : 1 + t], refs[1 + t]
    shard = ids[1]
    for i in range(n):
        attn_ref[:, i * HEAD_DIM : (i + 1) * HEAD_DIM] = heads_ref[i]
    total[...] = dot(attn_ref[...], w_ref[...], 1, 0).astype(BF16)
    rows = outs[0].shape[0]
    for i in range(t):
        outs[i][...] = total[pl.ds(offset(shard ^ i, rows), rows), :]


def lookup_kernel(t, ids, table_ref, w_ref, *refs):
    codes, outs, w_out_ref = refs[:t], refs[t : 2 * t], refs[2 * t]
    w_out_ref[...] = w_ref[...]
    book = pl.program_id(0)
    shard_rows, rows = table_ref.shape[1], codes[0].shape[0]
    picks = []
    for i in range(t):
        lanes = lax.broadcasted_iota(jnp.int32, codes[i].shape, 1)
        code = jnp.sum(jnp.where(lanes == book, codes[i][...], 0), axis=1, keepdims=True)
        entry = lax.broadcasted_iota(jnp.int32, (rows, shard_rows), 1) + ids[1] * shard_rows
        picks.append((entry == code).astype(F32).astype(BF16))
    found = dot(jnp.concatenate(picks, axis=0), table_ref[0], 1, 0).astype(BF16)
    for i in range(t):
        outs[i][0] = found[i * rows : (i + 1) * rows]


def depth_kernel(t, books, ids, gain_ref, embed_ref, up_ref, *refs):
    parts = refs[:t]
    depth_ref, sum_ref = refs[t:]
    projected = parts[0][...].astype(F32)
    for i in range(1, t):
        projected = projected + parts[i][...].astype(F32)
    gain = gain_ref[...]
    grad_sum = jnp.zeros_like(projected)
    gain_sum = jnp.zeros_like(projected)
    for book in range(books):
        hidden = projected + embed_ref[book].astype(F32)
        inverse = lax.rsqrt(jnp.mean(hidden * hidden, axis=1, keepdims=True) + EPSILON)
        normed = hidden * inverse
        depth_ref[book] = (normed * gain).astype(BF16)
        cotangent = up_ref[book].astype(F32)
        gain_sum = gain_sum + cotangent * normed
        grad = cotangent * gain
        grad_sum = grad_sum + inverse * (grad - normed * jnp.mean(grad * normed, axis=1, keepdims=True))
    rows = grad_sum.shape[0]
    sum_ref[:rows, :] = grad_sum.astype(BF16)
    sum_ref[rows:, :] = two_parts(jnp.sum(gain_sum, axis=0, keepdims=True), 0, sum_ref.shape[0] - rows)


def two_parts(row, slot, count):
    high = row.astype(BF16).astype(F32)
    place = lax.broadcasted_iota(jnp.int32, (count, row.shape[1]), 0)
    return jnp.where(place == 2 * slot, high, jnp.where(place == 2 * slot + 1, row - high, 0.0)).astype(BF16)


def grad_attn_kernel(n, t, ids, w_ref, *refs):
    parts, out_ref, keep_ref, send_ref, sum_s = refs[:t], refs[t], refs[t + 1], refs[t + 2], refs[t + 3]
    me, shard = ids[0], ids[1]
    rows = sum_s.shape[0] // t
    total = sum_s.shape[0]
    columns = keep_ref.shape[2]
    gain = jnp.zeros((1, sum_s.shape[1]), F32)
    for i in range(t):
        sum_s[pl.ds(offset(shard ^ i, rows), rows), :] = parts[i][:rows, :]
        gain = gain + jnp.sum(parts[i][rows:, :].astype(F32), axis=0, keepdims=True)
    grad = dot(sum_s[...], w_ref[...], 1, 1).astype(BF16)
    for i in range(n):
        out_ref[i] = grad[:, i * HEAD_DIM : (i + 1) * HEAD_DIM]
    core = me & 1
    gains = two_parts(gain, core, 2 * GAIN_SLOTS)
    for i in range(n // 2):
        even = slice(2 * i * columns, (2 * i + 1) * columns)
        odd = slice((2 * i + 1) * columns, (2 * i + 2) * columns)
        for ref, flip in ((keep_ref, core), (send_ref, 1 - core)):
            ref[i, :total, :] = jnp.where(flip == 0, sum_s[:, even], sum_s[:, odd])
            ref[i, total:, :] = jnp.where(flip == 0, gains[:, even], gains[:, odd])


def halving_order(n):
    order = [0]
    step = n // 2
    while step:
        order = order + [k + step for k in order]
        step //= 2
    return order


def grad_proj_kernel(n, ids, attn_ref, other_attn_ref, sum_ref, other_sum_ref, keep_ref, send_ref):
    chip = lax.shift_right_logical(ids[0], 1)
    rows, width = attn_ref.shape
    half = n // 4
    for i, k in enumerate(halving_order(n // 2)):
        term = dot(attn_ref[...], sum_ref[chip ^ k, :rows, :], 0, 0)
        term = term + dot(other_attn_ref[...], other_sum_ref[chip ^ k, :rows, :], 0, 0)
        tails = sum_ref[chip ^ k, rows:, :].astype(F32) + other_sum_ref[chip ^ k, rows:, :].astype(F32)
        gain = jnp.sum(tails, axis=0, keepdims=True)
        out_ref = keep_ref if i < half else send_ref
        out_ref[i % half, :width, :] = term.astype(BF16)
        out_ref[i % half, width:, :] = two_parts(gain, ids[0], 2 * n)


def pair_sum_kernel(ids, kept_ref, taken_ref, keep_ref, send_ref):
    half = keep_ref.shape[0]
    keep_ref[...] = kept_ref[:half].astype(F32) + taken_ref[:half].astype(F32)
    send_ref[...] = (kept_ref[half:].astype(F32) + taken_ref[half:].astype(F32)).astype(BF16)


def assemble_kernel(n, ids, pieces_ref, *outs):
    for i in range(n):
        for part in range(3):
            outs[part][:, i * HEAD_DIM : (i + 1) * HEAD_DIM] = pieces_ref[i, part].astype(F32)


def swap(x, axis, count, i):
    return lax.ppermute(x, axis, [(b, b ^ i) for b in range(count)])


def swap_all(parts, axis, count):
    moved = {0: parts[0]}
    for i in sorted(range(1, count), key=lambda i: (-(i.bit_length()), i)):
        moved[i] = swap(parts[i], axis, count, i)
    return [moved[i] for i in range(count)]


def heads_body(n, t, queries, key_rows, value_rows, segment_ids, codebook_ids, code_table, input_proj, norm_gain, upstream):
    rows, width = queries.shape
    frames = segment_ids.shape[0]
    books, shard_rows, depth = code_table.shape
    local = codebook_ids.shape[0]
    window = -(-(frames // 2 - 1) // rows)
    scale = HEAD_DIM ** (-0.5)
    factor = scale * LOG2_E
    ids = jnp.stack([lax.axis_index("ctx"), lax.axis_index("tp")]).astype(jnp.int32)
    seg = segment_ids.reshape(1, frames)
    piece = (3, rows, HEAD_DIM)
    tall = (frames, HEAD_DIM)

    (packed,) = call(
        functools.partial(pack_kernel, n),
        "pack",
        jnp.zeros((2,), jnp.int32),
        [queries, key_rows, value_rows],
        [((n,) + piece, BF16)],
        [pltpu.SemaphoreType.DMA((3 * n,))],
        in_specs={i: pl.BlockSpec(memory_space=pl.ANY) for i in range(3)},
        vmem=58,
    )
    pieces = lax.all_to_all(packed, "ctx", 0, 0, tiled=True)

    codes = [codebook_ids] + [swap(codebook_ids, "tp", t, i) for i in range(1, t)]
    found = call(
        functools.partial(lookup_kernel, t),
        "lookup",
        ids,
        [code_table, input_proj] + codes,
        [((books, local, depth), BF16)] * t + [((width, depth), BF16)],
        in_specs={
            0: pl.BlockSpec((1, shard_rows, depth), lambda step, ids: (step, 0, 0)),
            1: pl.BlockSpec((width // books, depth), lambda step, ids: (ids[1] * books + step, 0)),
        },
        out_specs={i: pl.BlockSpec((1, local, depth), lambda step, ids: (step, 0, 0)) for i in range(t)}
        | {t: pl.BlockSpec((width // books, depth), lambda step, ids: (step, 0))},
        grid=(books,),
        vmem=58,
        flops=2 * books * t * local * shard_rows * depth,
    )
    w_part = found[t]
    embedded = sum(x.astype(F32) for x in swap_all(found[:t], "tp", t)).astype(BF16)
    cotangent = upstream.transpose(1, 0, 2)

    pair_flops = 4 * frames * (window + 1) * rows * HEAD_DIM
    out_full, norm = call(
        functools.partial(forward_kernel, n, rows, window, factor),
        "attend",
        ids,
        [seg, pieces],
        [(tall, BF16), ((1, frames), F32)],
        flops=pair_flops,
        vmem=24,
    )
    out_heads = lax.all_to_all(out_full.reshape(n, rows, HEAD_DIM), "ctx", 0, 0, tiled=True)
    projected = call(
        functools.partial(project_kernel, n, t),
        "project",
        ids,
        [w_part, out_heads],
        [((rows, width), BF16)] + [((local, depth), BF16)] * t,
        [pltpu.VMEM((rows, depth), BF16)],
        flops=2 * rows * width * depth,
    )
    attn_out = projected[0]
    extra_rows = 8
    depth_rows, grad_sum = call(
        functools.partial(depth_kernel, t, books),
        "depth",
        ids,
        [norm_gain.reshape(1, depth), embedded, cotangent] + swap_all(projected[1:], "tp", t),
        [((books, local, depth), BF16), ((local + extra_rows, depth), BF16)],
    )
    sums = [grad_sum] + [swap(grad_sum, "tp", t, i) for i in range(1, t)]
    chunk = (n // 2, rows + 2 * GAIN_SLOTS, depth // n)
    grad_heads, sums_kept, sums_sent = call(
        functools.partial(grad_attn_kernel, n, t),
        "grad_attn",
        ids,
        [w_part] + sums,
        [((n, rows, HEAD_DIM), BF16), (chunk, BF16), (chunk, BF16)],
        [pltpu.VMEM((rows, depth), BF16)],
        flops=2 * rows * width * depth,
    )
    grad_full = lax.all_to_all(grad_heads, "ctx", 0, 0, tiled=True).reshape(tall)
    late_norm, _ = lax.optimization_barrier((norm, grad_heads))
    pair_rows = rows * sum(min(block, window) + 1 for block in range(n))
    (probs,) = call(
        functools.partial(probs_kernel, n, rows, window, factor),
        "probs",
        ids,
        [seg, late_norm, pieces],
        [((pair_rows, rows), BF16)],
        flops=pair_flops // 2,
        vmem=12,
    )
    attn_out, probs = lax.optimization_barrier((attn_out, probs))
    slab = (n // 4, width + 2 * n, depth // n)
    kept, sent = call(
        functools.partial(grad_proj_kernel, n),
        "grad_proj",
        ids,
        [attn_out, swap(attn_out, "ctx", n, 1), sums_kept, swap(sums_sent, "ctx", n, 1)],
        [(slab, BF16)] * 2,
        flops=2 * rows * width * depth,
    )
    sent, grad_full = lax.optimization_barrier((sent, grad_full))
    taken = swap(sent, "ctx", n, 2)
    (grads,) = call(
        functools.partial(backward_kernel, n, rows, window, scale),
        "attend_grad",
        ids,
        [probs, out_full, pieces, grad_full],
        [((n,) + piece, BF16)],
        [pltpu.VMEM(tall, F32)] * 2,
        costly=False,
        vmem=20,
    )
    step = 4
    while step < n:
        half = kept.shape[0] // 2
        kept, sent = call(
            pair_sum_kernel,
            "pair_sum",
            ids,
            [kept, taken],
            [((half,) + kept.shape[1:], F32), ((half,) + kept.shape[1:], BF16)],
            flops=1 << 36,
        )
        taken = swap(sent, "ctx", n, step)
        step *= 2
    back = lax.all_to_all(grads, "ctx", 0, 0, tiled=True)
    grad_query, grad_key, grad_value = call(
        functools.partial(assemble_kernel, n), "assemble", ids, [back], [((rows, width), F32)] * 3
    )
    taken, grad_query = lax.optimization_barrier((taken, grad_query))
    proj_sum = kept[0].astype(F32) + taken[0].astype(F32)
    grad_proj = proj_sum[:width]
    gain = jnp.sum(proj_sum[width:], axis=0)
    part = depth // (n * t)
    grad_gain = lax.dynamic_slice_in_dim(gain, lax.axis_index("tp") * part, part, 0)
    return (depth_rows.transpose(1, 0, 2), grad_query, grad_key, grad_value, grad_proj, grad_gain)


def body(n, t, queries, *rest):
    heads = queries.shape[1] // HEAD_DIM
    if heads == n and n & (n - 1) == 0 and t & (t - 1) == 0 and n > 3:
        return heads_body(n, t, queries, *rest)
    return general_body(queries, *rest)


def general_body(
    queries,
    key_rows,
    value_rows,
    segment_ids,
    codebook_ids,
    code_table,
    input_proj,
    norm_gain,
    upstream,
):
    local_rows = queries.shape[0]
    local_width = queries.shape[1]
    head_count = local_width // HEAD_DIM
    score_scale = HEAD_DIM ** (-0.5)
    ctx_index = lax.axis_index("ctx")
    tp_index = lax.axis_index("tp")
    all_keys, all_values = (
        lax.all_gather(key_rows, "ctx", axis=0, tiled=True),
        lax.all_gather(value_rows, "ctx", axis=0, tiled=True),
    )
    key_total = all_keys.shape[0]
    block_rows = 512
    block_count = key_total // block_rows
    block_list = jnp.arange(block_count, dtype=jnp.int32)
    first_row = ctx_index * local_rows

    def block_scores(query_heads, query_pos, query_seg, block_index):
        key_start = block_index * block_rows
        key_block = lax.dynamic_slice_in_dim(all_keys, key_start, block_rows, 0).reshape(
            block_rows, head_count, HEAD_DIM
        )
        value_block = lax.dynamic_slice_in_dim(all_values, key_start, block_rows, 0).reshape(
            block_rows, head_count, HEAD_DIM
        )
        scores = (
            jnp.einsum("qhd,khd->hqk", query_heads, key_block, preferred_element_type=jnp.float32)
            * score_scale
        )
        key_pos = key_start + jnp.arange(block_rows)
        key_seg = lax.dynamic_slice_in_dim(segment_ids, key_start, block_rows)
        allowed = (key_pos[None, :] <= query_pos[:, None]) & (
            key_seg[None, :] == query_seg[:, None]
        )
        return (jnp.where(allowed[None], scores, NEGATIVE), allowed, key_block, value_block)

    def visit(block_index, last_visible, carried, compute, skipped):
        return lax.cond(block_index * block_rows <= last_visible, compute, skipped, carried)

    def keep_state(state):
        return state

    def describe(query_rows, start_row):
        row_count = query_rows.shape[0]
        query_heads = query_rows.reshape(row_count, head_count, HEAD_DIM)
        query_pos = start_row + jnp.arange(row_count)
        query_seg = lax.dynamic_slice_in_dim(segment_ids, start_row, row_count)
        return (query_heads, query_pos, query_seg, start_row + row_count - 1)

    row_count = queries.shape[0]
    query_heads, query_pos, query_seg, last_visible = describe(queries, first_row)

    def stats_step(carried, block_index):

        def compute(state):
            top_score, row_mass = state
            scores, allowed, key_block, value_block = block_scores(
                query_heads, query_pos, query_seg, block_index
            )
            new_top = jnp.maximum(top_score, jnp.max(scores, axis=2))
            shifted = jnp.where(allowed[None], jnp.exp(scores - new_top[:, :, None]), 0.0)
            return (
                (new_top, row_mass * jnp.exp(top_score - new_top) + jnp.sum(shifted, axis=2)),
                scores,
            )

        def skipped(state):
            return (state, jnp.full((head_count, row_count, block_rows), NEGATIVE, jnp.float32))

        return visit(block_index, last_visible, carried, compute, skipped)

    start_top = jnp.full((head_count, row_count), NEGATIVE, jnp.float32)
    start_mass = jnp.zeros((head_count, row_count), jnp.float32)
    (top_score, row_mass), score_stack = lax.scan(stats_step, (start_top, start_mass), block_list)
    log_norm = top_score + jnp.log(row_mass)

    def output_step(carried, inputs):
        block_index, scores = inputs

        def compute(state):
            key_start = block_index * block_rows
            value_block = lax.dynamic_slice_in_dim(all_values, key_start, block_rows, 0).reshape(
                block_rows, head_count, HEAD_DIM
            )
            weights = jnp.exp(scores - log_norm[:, :, None]).astype(jnp.bfloat16)
            return state + jnp.einsum(
                "hqk,khd->qhd", weights, value_block, preferred_element_type=jnp.float32
            )

        return (visit(block_index, last_visible, carried, compute, keep_state), None)

    start_out = jnp.zeros((row_count, head_count, HEAD_DIM), jnp.float32)
    out_sum, unused = lax.scan(output_step, start_out, (block_list, score_stack))
    group_out = out_sum.reshape(row_count, local_width).astype(jnp.bfloat16)
    attn_out, log_norm = (group_out, log_norm)
    group_codes = lax.all_gather(codebook_ids, "tp", axis=0, tiled=True)
    shard_rows = code_table.shape[1]
    local_codes = group_codes - tp_index * shard_rows
    table_rows = jnp.arange(shard_rows, dtype=jnp.int32)
    selector = (local_codes[:, :, None] == table_rows[None, None, :]).astype(jnp.bfloat16)
    looked = jnp.einsum("tcr,crw->tcw", selector, code_table, preferred_element_type=jnp.float32)
    embedded = lax.psum_scatter(
        looked.astype(jnp.bfloat16), "tp", scatter_dimension=0, tiled=True
    ).astype(jnp.float32)
    w_part = lax.dynamic_slice_in_dim(input_proj, tp_index * local_width, local_width, 0)
    projected = lax.psum_scatter(
        jnp.dot(attn_out, w_part, preferred_element_type=jnp.float32).astype(jnp.bfloat16),
        "tp",
        scatter_dimension=0,
        tiled=True,
    ).astype(jnp.float32)
    hidden = projected[:, None, :] + embedded
    inverse = lax.rsqrt(jnp.mean(hidden * hidden, axis=2, keepdims=True) + EPSILON)
    normed = hidden * inverse
    depth_out = (normed * norm_gain).astype(jnp.bfloat16)
    cotangent = upstream.astype(jnp.float32)
    gain_term = jnp.sum(cotangent * normed, axis=(0, 1))
    grad_gain = lax.psum_scatter(gain_term, ("ctx", "tp"), scatter_dimension=0, tiled=True)
    grad_normed = cotangent * norm_gain
    grad_hidden = inverse * (
        grad_normed - normed * jnp.mean(grad_normed * normed, axis=2, keepdims=True)
    )
    grad_sum = jnp.sum(grad_hidden, axis=1).astype(jnp.bfloat16)
    gathered = lax.all_gather(grad_sum, "tp", axis=0, tiled=True)
    grad_attn = lax.dot_general(
        gathered, w_part, (((1,), (1,)), ((), ())), preferred_element_type=jnp.float32
    ).astype(jnp.bfloat16)
    weight_term = lax.dot_general(
        attn_out, gathered, (((0,), (0,)), ((), ())), preferred_element_type=jnp.float32
    )
    grad_proj = lax.psum_scatter(
        weight_term.astype(jnp.bfloat16), "ctx", scatter_dimension=1, tiled=True
    ).astype(jnp.float32)
    backward_row_count = queries.shape[0]
    backward_query_heads, backward_query_pos, backward_query_seg, backward_last_visible = describe(
        queries, first_row
    )
    grad_heads = grad_attn.reshape(backward_row_count, head_count, HEAD_DIM)
    out_heads = attn_out.reshape(backward_row_count, head_count, HEAD_DIM)
    row_delta = jnp.sum(grad_heads.astype(jnp.float32) * out_heads.astype(jnp.float32), axis=2).T

    def back_step(carried, block_index):

        def compute(query_total):
            scores, allowed, key_block, value_block = block_scores(
                backward_query_heads, backward_query_pos, backward_query_seg, block_index
            )
            probs = jnp.exp(scores - log_norm[:, :, None])
            weights = probs.astype(jnp.bfloat16)
            grad_prob = jnp.einsum(
                "qhd,khd->hqk", grad_heads, value_block, preferred_element_type=jnp.float32
            )
            grad_score = (probs * (grad_prob - row_delta[:, :, None])).astype(jnp.bfloat16)
            query_total = query_total + jnp.einsum(
                "hqk,khd->qhd", grad_score, key_block, preferred_element_type=jnp.float32
            )
            key_grad = (
                jnp.einsum(
                    "hqk,qhd->khd",
                    grad_score,
                    backward_query_heads,
                    preferred_element_type=jnp.float32,
                )
                * score_scale
            )
            value_grad = jnp.einsum(
                "hqk,qhd->khd", weights, grad_heads, preferred_element_type=jnp.float32
            )
            return (
                query_total,
                (
                    key_grad.reshape(block_rows, local_width),
                    value_grad.reshape(block_rows, local_width),
                ),
            )

        def skipped(query_total):
            empty_block = jnp.zeros((block_rows, local_width), jnp.float32)
            return (query_total, (empty_block, empty_block))

        return visit(block_index, backward_last_visible, carried, compute, skipped)

    start_grad = jnp.zeros((backward_row_count, head_count, HEAD_DIM), jnp.float32)
    query_sum, (key_stack, value_stack) = lax.scan(back_step, start_grad, block_list)
    group_query = (query_sum * score_scale).reshape(backward_row_count, local_width)
    key_acc = key_stack.reshape(key_total, local_width)
    value_acc = value_stack.reshape(key_total, local_width)
    grad_key, grad_value = (
        lax.psum_scatter(
            key_acc.astype(jnp.bfloat16), "ctx", scatter_dimension=0, tiled=True
        ).astype(jnp.float32),
        lax.psum_scatter(
            value_acc.astype(jnp.bfloat16), "ctx", scatter_dimension=0, tiled=True
        ).astype(jnp.float32),
    )
    return (depth_out, group_query, grad_key, grad_value, grad_proj, grad_gain)


def solution(mesh):
    return jax.shard_map(
        functools.partial(body, mesh.shape["ctx"], mesh.shape["tp"]),
        mesh=mesh,
        in_specs=(
            P("ctx", "tp"),
            P("ctx", "tp"),
            P("ctx", "tp"),
            P(),
            P(("ctx", "tp"), None),
            P(None, "tp", None),
            P(),
            P(),
            P(("ctx", "tp"), None, None),
        ),
        out_specs=(
            P(("ctx", "tp"), None, None),
            P("ctx", "tp"),
            P("ctx", "tp"),
            P("ctx", "tp"),
            P("tp", "ctx"),
            P(("ctx", "tp")),
        ),
        check_vma=False,
    )
```
